512 devices in a mesh: grp: 16 (over x_lo, y, core), dev: 32 (over x_hi, z).
Axes of the slice: x: 4 (x_hi: 2, x_lo: 2; x = x_hi * 2 + x_lo), y: 4, z: 16, core: 2. Of those that a mesh axis runs over, the one named last changes fastest.
Arguments:
- voltage: float32 [2, 4096, 4192], P(None, ('grp', 'dev')), may hold values from -6 to 6
- filter_taps: float32 [4, 32], replicated, may hold values from -0.5 to 0.5
- plan: int32 [16, 9], P('grp'), may hold values from 0 to 8, each once within a row
Outputs:
- visibility: bfloat16 [16, 9, 32, 2, 256, 256], P('grp', None, 'dev')
The draws below stay inside these ranges and needn't reach their ends.
Inputs may be any that keep to these rules, and one draw needn't show every extreme that they name: Each row of plan holds every distance 0 to 8 once.
All inputs are finite; a program needn't handle non-finite values.
Results may differ from the reference program's by a relative error of at most 0.0056.
Values may be sent and summed in bfloat16 or wider, within the bound.
No kernel may reach another device: no remote copies, remote signals or barrier semaphores. Data moves between devices by JAX's collectives and lax.ppermute only.
A program may use at most 64 MiB of HBM per device.

```python
import math
import jax
import jax.numpy as jnp
from jax import lax

F = 32
TAPS = 4
SPECTRA = 128
INPUTS = 4096
BLK = 256
ROUNDS = 9
FRAMES = 131
N_GRP = 16


def steps_of(key, dims, shards, least, largest):
    def one(axis_at, blocks):
        draws = jax.random.uniform(jax.random.fold_in(jax.random.fold_in(key, 6), axis_at), (blocks,), jnp.float32, least / len(shards), largest / len(shards))
        return jnp.repeat(jnp.exp(draws), dims[axis_at] // blocks).reshape((-1,) + (1,) * (len(dims) - axis_at - 1))

    factor_of = one(*shards[0])
    for cut in shards[1:]:
        factor_of = factor_of * one(*cut)
    return factor_of


def bell_draw(stream_key, dims, scale, reach, split=(), kind=jnp.bfloat16):
    result = scale * jax.random.normal(stream_key, dims, jnp.float32)
    if split:
        result = result * steps_of(stream_key, dims, split, -0.22, 0.18)
    return jnp.clip(result, -reach, reach).astype(kind)


def setup_inputs(seed: int = 0) -> dict:
    key_list = jax.random.split(jax.random.key(seed), 4)
    voltage = bell_draw(key_list[0], (2, INPUTS, FRAMES * F), 1.0, 6.0, ((1, 512),), jnp.float32)
    filter_taps = bell_draw(key_list[1], (TAPS, F), (TAPS * F) ** -0.5, 0.5, (), jnp.float32)
    plan = jax.vmap(lambda own: jax.random.permutation(own, ROUNDS))(jax.random.split(key_list[2], N_GRP)).reshape((N_GRP, ROUNDS)).astype(jnp.int32)
    return {"voltage": voltage, "filter_taps": filter_taps, "plan": plan}


def compute_spectra(voltage, filter_taps):
    signal_input_count = voltage.shape[1]
    framed_samples = voltage.reshape(2, signal_input_count, FRAMES, F)
    filtered = filter_taps[0][None, None, None, :] * framed_samples[:, :, 0:SPECTRA, :]
    for p in range(1, TAPS):
        filtered = filtered + filter_taps[p][None, None, None, :] * framed_samples[:, :, p:p + SPECTRA, :]
    indices = jnp.arange(F, dtype=jnp.int32)
    phase_angle = ((indices[:, None] * indices[None, :]) % F).astype(jnp.float32) * (2.0 * math.pi / F)
    cosine_table = jnp.cos(phase_angle)
    sine_table = jnp.sin(phase_angle)
    highest = lax.Precision.HIGHEST
    real_part = jnp.einsum('csn,nf->fcs', filtered[0], cosine_table, precision=highest) + jnp.einsum('csn,nf->fcs', filtered[1], sine_table, precision=highest)
    imaginary_component = jnp.einsum('csn,nf->fcs', filtered[1], cosine_table, precision=highest) - jnp.einsum('csn,nf->fcs', filtered[0], sine_table, precision=highest)
    return jnp.stack([real_part, imaginary_component], axis=2).astype(jnp.bfloat16)


def correlate(own_block, partner):
    chans, rows_here = own_block.shape[0], own_block.shape[1]
    left_spectrum_rows = own_block.reshape(chans, rows_here, -1).astype(jnp.float32)
    real_part = partner[:, :, 0, :]
    imaginary_component = partner[:, :, 1, :]
    right_spectrum_rows = jnp.stack([jnp.concatenate([real_part, imaginary_component], -1), jnp.concatenate([-imaginary_component, real_part], -1)], axis=1).astype(jnp.float32)
    cross_products = jnp.einsum('gzi,gkvi->gkzv', left_spectrum_rows, right_spectrum_rows)
    return (cross_products / SPECTRA).astype(jnp.bfloat16)


def reference(voltage, filter_taps, plan):
    spectra = compute_spectra(voltage, filter_taps)
    blocks = spectra.reshape(F, N_GRP, BLK, 2, SPECTRA).transpose(1, 0, 2, 3, 4)
    results = []
    for distance in range(ROUNDS):
        partner = jnp.roll(blocks, distance, axis=0)
        results.append(lax.map(lambda operands: correlate(operands[0], operands[1]), (blocks, partner)))
    stacked = jnp.stack(results, axis=1)
    picks = plan.astype(jnp.int32)[:, :, None, None, None, None]
    return jnp.take_along_axis(stacked, picks, axis=1)
```

```python
import math

import jax
import jax.numpy as jnp
import numpy as np
from jax import lax
from jax.experimental import pallas as pl
from jax.experimental.pallas import tpu as pltpu
from jax.sharding import Mesh, PartitionSpec as P

F = 32
TAPS = 4
SPECTRA = 128
FRAMES = 131
HERE = 8
LANES = 128
TILES = 33
BLOCK = (32, 2, HERE, SPECTRA)


def dft_table():
    f = np.arange(F)[:, None]
    n = np.arange(F)[None, :]
    angle = 2.0 * math.pi * ((f * n) % F) / F
    cosine = np.tile(np.cos(angle), (1, TAPS))
    sine = np.tile(np.sin(angle), (1, TAPS))
    real_rows = np.concatenate([cosine, sine], axis=1)
    imag_rows = np.concatenate([-sine, cosine], axis=1)
    return np.concatenate([real_rows, imag_rows], axis=0).astype(np.float32)


def split(x):
    high = x.astype(jnp.bfloat16)
    low = (x - high.astype(jnp.float32)).astype(jnp.bfloat16)
    return high, low


def nt(a, b):
    return lax.dot_general(a, b, (((1,), (1,)), ((), ())), preferred_element_type=jnp.float32)


def spectra_kernel(v_ref, taps_ref, table_ref, out_ref, rows, placed):
    for c in range(2):
        for q in range(TILES - 1):
            rows[c, q * HERE : (q + 1) * HERE, :] = v_ref[c, :, q * LANES : (q + 1) * LANES]
        rows[c, (TILES - 1) * HERE :, : FRAMES * F - (TILES - 1) * LANES] = v_ref[
            c, :, (TILES - 1) * LANES :
        ]
    taps = taps_ref[...]
    tap_row = jnp.concatenate([taps[p : p + 1, :] for p in range(TAPS)], axis=1)
    weights = table_ref[...] * jnp.concatenate([tap_row, tap_row], axis=1)
    w_high, w_low = split(weights)
    w_both = jnp.concatenate([w_high, w_low], axis=0)
    lane = lax.broadcasted_iota(jnp.int32, (F, LANES), 1)
    for i in range(HERE):
        halves = []
        for c in range(2):
            here = rows[c, pl.ds(i, 32, stride=HERE), :]
            after = rows[c, pl.ds(i + HERE, 32, stride=HERE), :]
            parts = [here]
            for j in range(1, 4):
                parts.append(pltpu.roll(jnp.where(lane < F * j, after, here), LANES - F * j, 1))
            halves.append(jnp.concatenate(parts, axis=0))
        x_high, x_low = split(jnp.concatenate(halves, axis=1))
        both = nt(w_both, x_high)
        result = both[: 2 * F] + both[2 * F :] + nt(w_high, x_low)
        placed[pl.ds(i, F, stride=2 * HERE), :] = result[:F]
        placed[pl.ds(HERE + i, F, stride=2 * HERE), :] = result[F:]
    values = placed[...].astype(jnp.bfloat16).reshape(2, 16, 2, HERE, SPECTRA)
    out_ref[:, 0] = values[0]
    out_ref[:, 1] = values[1]


def compute_spectra(voltage, filter_taps):
    return pl.pallas_call(
        spectra_kernel,
        out_shape=jax.ShapeDtypeStruct((16, 2, 2, HERE, SPECTRA), jnp.bfloat16),
        in_specs=[pl.BlockSpec(memory_space=pltpu.VMEM)] * 3,
        out_specs=pl.BlockSpec(memory_space=pltpu.VMEM),
        scratch_shapes=[
            pltpu.VMEM((2, TILES * HERE, LANES), jnp.float32),
            pltpu.VMEM((F * 2 * HERE, SPECTRA), jnp.float32),
        ],
        cost_estimate=pl.CostEstimate(flops=10**8, bytes_accessed=400000, transcendentals=0),
        name="spectra",
    )(voltage, filter_taps, jnp.asarray(dft_table()))


def correlate_kernel(count, first, slots_ref, own_ref, partners_ref, *rest):
    out_ref, staged, sems = rest[-3:]
    own = own_ref[...]
    left = jnp.concatenate(
        [own[:, 0].reshape(256, SPECTRA), own[:, 1].reshape(256, SPECTRA)], axis=1
    )
    copies = []
    for b in range(count):
        real_part = partners_ref[b, :, 0].reshape(256, SPECTRA)
        imag_part = partners_ref[b, :, 1].reshape(256, SPECTRA)
        scale = 1.0 / SPECTRA
        staged[b, 0] = (
            nt(left, jnp.concatenate([real_part, imag_part], axis=1)) * scale
        ).astype(jnp.bfloat16)
        staged[b, 1] = (
            nt(left, jnp.concatenate([-imag_part, real_part], axis=1)) * scale
        ).astype(jnp.bfloat16)
        copy = pltpu.make_async_copy(staged.at[b], out_ref.at[slots_ref[first + b]], sems.at[b])
        copy.start()
        copies.append(copy)
    for copy in copies:
        copy.wait()


def correlate(slots, first, own, partners, before=None):
    count = partners.shape[0]
    operands = [slots, own, partners]
    in_specs = [
        pl.BlockSpec(memory_space=pltpu.SMEM),
        pl.BlockSpec(memory_space=pltpu.VMEM),
        pl.BlockSpec(memory_space=pltpu.VMEM),
    ]
    aliases = {}
    if before is not None:
        operands.append(before)
        in_specs.append(pl.BlockSpec(memory_space=pl.ANY))
        aliases = {3: 0}

    def kernel(*refs):
        correlate_kernel(count, first, *refs)

    return pl.pallas_call(
        kernel,
        out_shape=jax.ShapeDtypeStruct((9, 2, 256, 256), jnp.bfloat16),
        in_specs=in_specs,
        out_specs=pl.BlockSpec(memory_space=pl.ANY),
        scratch_shapes=[
            pltpu.VMEM((count, 2, 256, 256), jnp.bfloat16),
            pltpu.SemaphoreType.DMA((count,)),
        ],
        input_output_aliases=aliases,
        cost_estimate=pl.CostEstimate(
            flops=count * 2**26, bytes_accessed=count * 400000, transcendentals=0
        ),
        name="correlate",
    )(*operands)


def per_device(voltage, filter_taps, plan):
    x_lo, y, core = lax.axis_index("x_lo"), lax.axis_index("y"), lax.axis_index("core")
    spectra = compute_spectra(voltage, filter_taps)

    rows = jnp.arange(4, dtype=jnp.int32)
    steps = (y - rows) % 4
    other_core = jnp.where(core == 0, jnp.where(steps == 0, 7, 2 * steps - 1), 2 * steps + 1)
    others = (y - jnp.arange(1, 4, dtype=jnp.int32)) % 4
    distances = jnp.concatenate(
        [jnp.array([0, 8, 2, 4, 6], jnp.int32), other_core]
    )
    slots = jnp.sum(
        jnp.where(
            plan[0][None, :] == distances[:, None], jnp.arange(9, dtype=jnp.int32)[None, :], 0
        ),
        axis=1,
    )

    by_z = lax.all_to_all(spectra, "z", split_axis=0, concat_axis=0, tiled=True)
    by_x_hi = jnp.moveaxis(by_z, 1, 0)
    to_x = jnp.stack([by_x_hi, by_x_hi]).reshape(4, *by_x_hi.shape[1:])
    along_x = lax.all_to_all(to_x, ("x_lo", "x_hi"), split_axis=0, concat_axis=0, tiled=True)
    pair = along_x.reshape(2, *BLOCK)
    own = lax.dynamic_index_in_dim(pair, x_lo, 0, keepdims=False)
    across = lax.dynamic_index_in_dim(pair, 1 - x_lo, 0, keepdims=False)

    own_there = (rows > y) | ((rows == y) & (core == 0))
    to_y = jnp.where(own_there[:, None, None, None, None], own[None], across[None])
    along_y = lax.all_to_all(to_y, "y", split_axis=0, concat_axis=0, tiled=True)
    out = correlate(slots, 0, own, jnp.stack([own, across]))

    swapped = lax.ppermute(along_y, "core", [(0, 1), (1, 0)])
    out = correlate(slots, 2, own, along_y[others], out)
    out = correlate(slots, 5, own, swapped, out)
    return out[None, :, None]


def solution(mesh):
    fine = Mesh(mesh.devices.reshape(2, 4, 2, 2, 16), ("x_lo", "y", "core", "x_hi", "z"))
    grp, dev = ("x_lo", "y", "core"), ("x_hi", "z")
    return jax.shard_map(
        per_device,
        mesh=fine,
        in_specs=(P(None, grp + dev, None), P(), P(grp, None)),
        out_specs=P(grp, None, dev, None, None, None),
        check_vma=False,
    )
```

```python
import math

import jax
import jax.numpy as jnp
import numpy as np
from jax import lax
from jax.experimental import pallas as pl
from jax.experimental.pallas import tpu as pltpu
from jax.sharding import PartitionSpec as P

F = 32
TAPS = 4
SPECTRA = 128
FRAMES = 131
HERE = 8
LANES = 128
TILES = 33
ROUNDS = 9
BLK = 256
BLOCK = (32, 2, HERE, SPECTRA)


def dft_table():
    f = np.arange(F)[:, None]
    n = np.arange(F)[None, :]
    angle = 2.0 * math.pi * ((f * n) % F) / F
    cosine = np.tile(np.cos(angle), (1, TAPS))
    sine = np.tile(np.sin(angle), (1, TAPS))
    real_rows = np.concatenate([cosine, sine], axis=1)
    imag_rows = np.concatenate([-sine, cosine], axis=1)
    return np.concatenate([real_rows, imag_rows], axis=0).astype(np.float32)


def split(x):
    high = x.astype(jnp.bfloat16)
    low = (x - high.astype(jnp.float32)).astype(jnp.bfloat16)
    return high, low


def nt(a, b):
    return lax.dot_general(a, b, (((1,), (1,)), ((), ())), preferred_element_type=jnp.float32)


def spectra_kernel(v_ref, taps_ref, table_ref, out_ref, rows, placed):
    for c in range(2):
        for q in range(TILES - 1):
            rows[c, q * HERE : (q + 1) * HERE, :] = v_ref[c, :, q * LANES : (q + 1) * LANES]
        rows[c, (TILES - 1) * HERE :, : FRAMES * F - (TILES - 1) * LANES] = v_ref[
            c, :, (TILES - 1) * LANES :
        ]
    taps = taps_ref[...]
    tap_row = jnp.concatenate([taps[p : p + 1, :] for p in range(TAPS)], axis=1)
    weights = table_ref[...] * jnp.concatenate([tap_row, tap_row], axis=1)
    w_high, w_low = split(weights)
    w_both = jnp.concatenate([w_high, w_low], axis=0)
    lane = lax.broadcasted_iota(jnp.int32, (F, LANES), 1)
    for i in range(HERE):
        halves = []
        for c in range(2):
            here = rows[c, pl.ds(i, 32, stride=HERE), :]
            after = rows[c, pl.ds(i + HERE, 32, stride=HERE), :]
            parts = [here]
            for j in range(1, 4):
                parts.append(pltpu.roll(jnp.where(lane < F * j, after, here), LANES - F * j, 1))
            halves.append(jnp.concatenate(parts, axis=0))
        x_high, x_low = split(jnp.concatenate(halves, axis=1))
        both = nt(w_both, x_high)
        result = both[: 2 * F] + both[2 * F :] + nt(w_high, x_low)
        placed[pl.ds(i, F, stride=2 * HERE), :] = result[:F]
        placed[pl.ds(HERE + i, F, stride=2 * HERE), :] = result[F:]
    out_ref[...] = placed[...].astype(jnp.bfloat16).reshape(BLOCK)


def compute_spectra(voltage, filter_taps):
    return pl.pallas_call(
        spectra_kernel,
        out_shape=jax.ShapeDtypeStruct(BLOCK, jnp.bfloat16),
        in_specs=[pl.BlockSpec(memory_space=pltpu.VMEM)] * 3,
        out_specs=pl.BlockSpec(memory_space=pltpu.VMEM),
        scratch_shapes=[
            pltpu.VMEM((2, TILES * HERE, LANES), jnp.float32),
            pltpu.VMEM((F * 2 * HERE, SPECTRA), jnp.float32),
        ],
        cost_estimate=pl.CostEstimate(flops=10**8, bytes_accessed=400000, transcendentals=0),
        name="spectra",
    )(voltage, filter_taps, jnp.asarray(dft_table()))


def in_vmem(x):
    return pltpu.with_memory_space_constraint(x, pltpu.VMEM)


def correlate(plan, own, blocks, entries, before=None):
    count = len(entries)

    def kernel(plan_hbm, own_ref, *rest):
        block_refs, rest = rest[: len(blocks)], rest[len(blocks) :]
        out_ref, staged, plan_ref, plan_sem, sems = rest[-5:]
        fetch = pltpu.make_async_copy(plan_hbm, plan_ref, plan_sem)
        fetch.start()
        core = lax.axis_index("grp") % 2
        own = own_ref[...]
        left = jnp.concatenate(
            [own[:, 0].reshape(BLK, SPECTRA), own[:, 1].reshape(BLK, SPECTRA)], axis=1
        )
        copies = []
        for b, (array, index, distance, always) in enumerate(entries):
            ref = block_refs[array]
            real_part = ref[index, :, 0].reshape(BLK, SPECTRA)
            imag_part = ref[index, :, 1].reshape(BLK, SPECTRA)
            scale = 1.0 / SPECTRA
            staged[b, 0] = (
                nt(left, jnp.concatenate([real_part, imag_part], axis=1)) * scale
            ).astype(jnp.bfloat16)
            staged[b, 1] = (
                nt(left, jnp.concatenate([-imag_part, real_part], axis=1)) * scale
            ).astype(jnp.bfloat16)
            if b == 0:
                fetch.wait()
            wanted = distance(core)
            slot = jnp.int32(0)
            for r in range(ROUNDS):
                slot = jnp.where(plan_ref[0, r] == wanted, r, slot)
            copy = pltpu.make_async_copy(staged.at[b], out_ref.at[slot], sems.at[b])
            if always:
                copy.start()
            else:
                pl.when((wanted >= 0) & (wanted < ROUNDS))(copy.start)
            copies.append((copy, always, wanted))
        for copy, always, wanted in copies:
            if always:
                copy.wait()
            else:
                pl.when((wanted >= 0) & (wanted < ROUNDS))(copy.wait)

    operands = [plan, in_vmem(own), *[in_vmem(b) for b in blocks]]
    in_specs = [pl.BlockSpec(memory_space=pl.ANY)] + [pl.BlockSpec(memory_space=pltpu.VMEM)] * (
        1 + len(blocks)
    )
    aliases = {}
    if before is not None:
        aliases = {len(operands): 0}
        operands.append(before)
        in_specs.append(pl.BlockSpec(memory_space=pl.ANY))
    return pl.pallas_call(
        kernel,
        out_shape=jax.ShapeDtypeStruct((ROUNDS, 2, BLK, BLK), jnp.bfloat16),
        in_specs=in_specs,
        out_specs=pl.BlockSpec(memory_space=pl.ANY),
        scratch_shapes=[
            pltpu.VMEM((count, 2, BLK, BLK), jnp.bfloat16),
            pltpu.SMEM((1, ROUNDS), jnp.int32),
            pltpu.SemaphoreType.DMA,
            pltpu.SemaphoreType.DMA((count,)),
        ],
        input_output_aliases=aliases,
        cost_estimate=pl.CostEstimate(
            flops=count * 2**26, bytes_accessed=count * 400000, transcendentals=0
        ),
        name="correlate",
    )(*operands)


def per_device(voltage, filter_taps, plan):
    core = lax.axis_index("grp") % 2
    spectra = compute_spectra(voltage, filter_taps)
    own = lax.all_to_all(spectra, "dev", split_axis=0, concat_axis=0, tiled=True)

    def fetch(x, back):
        return lax.ppermute(
            x,
            "grp",
            [((2 * (chip - back - c)) % 16 + c, 2 * chip + c) for chip in range(8) for c in range(2)],
        )

    def swap(x):
        return lax.ppermute(x, "grp", [(g, g ^ 1) for g in range(16)])

    other = swap(own)
    pair = jnp.where(core == 0, jnp.stack([own, other]), jnp.stack([other, own]))
    near = fetch(pair, 1)
    far = fetch(pair, 3)
    near_swapped = swap(near)
    far_swapped = swap(far)

    def here(back, c):
        return lambda core: 2 * (back + core) + core - c

    def there(back, c):
        return lambda core: 2 * (back + 1 - core) + core - c

    out = correlate(
        plan, own, [pair], [(0, 0, lambda core: core, False), (0, 1, lambda core: core - 1, False)]
    )
    out = correlate(
        plan,
        own,
        [near, far],
        [(0, 0, here(1, 0), True), (0, 1, here(1, 1), True), (1, 0, here(3, 0), False), (1, 1, here(3, 1), True)],
        out,
    )
    out = correlate(
        plan,
        own,
        [near_swapped, far_swapped],
        [(0, 0, there(1, 0), True), (0, 1, there(1, 1), True), (1, 0, there(3, 0), True), (1, 1, there(3, 1), True)],
        out,
    )
    return out[None, :, None]


def solution(mesh):
    return jax.shard_map(
        per_device,
        mesh=mesh,
        in_specs=(P(None, ("grp", "dev"), None), P(), P("grp", None)),
        out_specs=P("grp", None, "dev", None, None, None),
        check_vma=False,
    )
```

```python
import math

import jax
import jax.numpy as jnp
import numpy as np
from jax import lax
from jax.experimental import pallas as pl
from jax.experimental.pallas import tpu as pltpu
from jax.sharding import Mesh, PartitionSpec as P

F = 32
TAPS = 4
SPECTRA = 128
FRAMES = 131
HERE = 8
LANES = 128
TILES = 33
ROUNDS = 9
BLK = 256
CHIPS = 8
BLOCK = (32, 2, HERE, SPECTRA)


def dft_table():
    f = np.arange(F)[:, None]
    n = np.arange(F)[None, :]
    angle = 2.0 * math.pi * ((f * n) % F) / F
    cosine = np.tile(np.cos(angle), (1, TAPS))
    sine = np.tile(np.sin(angle), (1, TAPS))
    real_rows = np.concatenate([cosine, sine], axis=1)
    imag_rows = np.concatenate([-sine, cosine], axis=1)
    return np.concatenate([real_rows, imag_rows], axis=0).astype(np.float32)


def split(x):
    high = x.astype(jnp.bfloat16)
    low = (x - high.astype(jnp.float32)).astype(jnp.bfloat16)
    return high, low


def nt(a, b):
    return lax.dot_general(a, b, (((1,), (1,)), ((), ())), preferred_element_type=jnp.float32)


def spectra_kernel(v_ref, taps_ref, table_ref, out_ref, rows, placed):
    for c in range(2):
        for q in range(TILES - 1):
            rows[c, q * HERE : (q + 1) * HERE, :] = v_ref[c, :, q * LANES : (q + 1) * LANES]
        rows[c, (TILES - 1) * HERE :, : FRAMES * F - (TILES - 1) * LANES] = v_ref[
            c, :, (TILES - 1) * LANES :
        ]
    taps = taps_ref[...]
    tap_row = jnp.concatenate([taps[p : p + 1, :] for p in range(TAPS)], axis=1)
    weights = table_ref[...] * jnp.concatenate([tap_row, tap_row], axis=1)
    w_high, w_low = split(weights)
    w_both = jnp.concatenate([w_high, w_low], axis=0)
    lane = lax.broadcasted_iota(jnp.int32, (F, LANES), 1)
    for i in range(HERE):
        halves = []
        for c in range(2):
            here = rows[c, pl.ds(i, 32, stride=HERE), :]
            after = rows[c, pl.ds(i + HERE, 32, stride=HERE), :]
            parts = [here]
            for j in range(1, 4):
                parts.append(pltpu.roll(jnp.where(lane < F * j, after, here), LANES - F * j, 1))
            halves.append(jnp.concatenate(parts, axis=0))
        x_high, x_low = split(jnp.concatenate(halves, axis=1))
        both = nt(w_both, x_high)
        result = both[: 2 * F] + both[2 * F :] + nt(w_high, x_low)
        placed[pl.ds(i, F, stride=2 * HERE), :] = result[:F]
        placed[pl.ds(HERE + i, F, stride=2 * HERE), :] = result[F:]
    values = placed[...].astype(jnp.bfloat16).reshape(2, 16, 2, HERE, SPECTRA)
    out_ref[:, 0] = values[0]
    out_ref[:, 1] = values[1]


def compute_spectra(voltage, filter_taps):
    return pl.pallas_call(
        spectra_kernel,
        out_shape=pltpu.VMEM((16, 2, 2, HERE, SPECTRA), jnp.bfloat16),
        in_specs=[pl.BlockSpec(memory_space=pltpu.VMEM)] * 3,
        out_specs=pl.BlockSpec(memory_space=pltpu.VMEM),
        scratch_shapes=[
            pltpu.VMEM((2, TILES * HERE, LANES), jnp.float32),
            pltpu.VMEM((F * 2 * HERE, SPECTRA), jnp.float32),
        ],
        cost_estimate=pl.CostEstimate(flops=10**8, bytes_accessed=400000, transcendentals=0),
        name="spectra",
    )(voltage, filter_taps, jnp.asarray(dft_table()))


def in_vmem(x):
    return pltpu.with_memory_space_constraint(x, pltpu.VMEM)


def spread_kernel(by_z_ref, out_ref):
    for x_hi in range(2):
        part = by_z_ref[:, x_hi]
        for chip in range(CHIPS):
            out_ref[chip, x_hi] = part


def spread(by_z):
    return pl.pallas_call(
        spread_kernel,
        out_shape=pltpu.VMEM((CHIPS, 2, 16, 2, HERE, SPECTRA), jnp.bfloat16),
        in_specs=[pl.BlockSpec(memory_space=pltpu.VMEM)],
        out_specs=pl.BlockSpec(memory_space=pltpu.VMEM),
        name="spread",
    )(in_vmem(by_z))


def my_chip():
    return 4 * lax.axis_index("x_lo") + lax.axis_index("y")


def stack_kernel(blocks_ref, out_ref):
    chip, core = my_chip(), lax.axis_index("core")
    for back in range(1, 4):
        out_ref[back - 1] = blocks_ref[(chip + CHIPS - back) % CHIPS]
    out_ref[3] = blocks_ref[(chip + 4 * core) % CHIPS]


def stack_for_swap(blocks):
    return pl.pallas_call(
        stack_kernel,
        out_shape=pltpu.VMEM((4, *BLOCK), jnp.bfloat16),
        in_specs=[pl.BlockSpec(memory_space=pltpu.VMEM)],
        out_specs=pl.BlockSpec(memory_space=pltpu.VMEM),
        name="stack_for_swap",
    )(in_vmem(blocks))


def correlate(plan, blocks, partners, entries, before=None):
    count = len(entries)

    def kernel(plan_in, blocks_ref, ref, *rest):
        out_ref, staged, plan_ref, plan_sem, sems = rest[-5:]
        fetch = pltpu.make_async_copy(plan_in, plan_ref, plan_sem)
        fetch.start()
        place = (my_chip(), lax.axis_index("core"))
        own = blocks_ref[place[0]]
        left = jnp.concatenate(
            [own[:, 0].reshape(BLK, SPECTRA), own[:, 1].reshape(BLK, SPECTRA)], axis=1
        )
        copies = []
        for b, entry in enumerate(entries):
            index, wanted = entry(*place)
            real_part = ref[index, :, 0].reshape(BLK, SPECTRA)
            imag_part = ref[index, :, 1].reshape(BLK, SPECTRA)
            scale = 1.0 / SPECTRA
            staged[b, 0] = (
                nt(left, jnp.concatenate([real_part, imag_part], axis=1)) * scale
            ).astype(jnp.bfloat16)
            staged[b, 1] = (
                nt(left, jnp.concatenate([-imag_part, real_part], axis=1)) * scale
            ).astype(jnp.bfloat16)
            if b == 0:
                fetch.wait()
            slot = jnp.int32(0)
            for r in range(ROUNDS):
                slot = jnp.where(plan_ref[0, r] == wanted, r, slot)
            copy = pltpu.make_async_copy(staged.at[b], out_ref.at[slot], sems.at[b])
            copy.start()
            copies.append(copy)
        for copy in copies:
            copy.wait()

    operands = [in_vmem(plan), in_vmem(blocks), in_vmem(partners)]
    in_specs = [pl.BlockSpec(memory_space=pltpu.VMEM)] * len(operands)
    aliases = {}
    if before is not None:
        aliases = {len(operands): 0}
        operands.append(before)
        in_specs.append(pl.BlockSpec(memory_space=pl.ANY))
    return pl.pallas_call(
        kernel,
        out_shape=jax.ShapeDtypeStruct((ROUNDS, 2, BLK, BLK), jnp.bfloat16),
        in_specs=in_specs,
        out_specs=pl.BlockSpec(memory_space=pl.ANY),
        scratch_shapes=[
            pltpu.VMEM((count, 2, BLK, BLK), jnp.bfloat16),
            pltpu.SMEM((1, ROUNDS), jnp.int32),
            pltpu.SemaphoreType.DMA,
            pltpu.SemaphoreType.DMA((count,)),
        ],
        input_output_aliases=aliases,
        cost_estimate=pl.CostEstimate(
            flops=count * 2**26, bytes_accessed=count * 400000, transcendentals=0
        ),
        name="correlate",
    )(*operands)


def per_device(voltage, filter_taps, plan):
    spectra = compute_spectra(voltage, filter_taps)
    by_z = lax.all_to_all(spectra, "z", split_axis=0, concat_axis=0, tiled=True)
    members = CHIPS * 2
    blocks = lax.all_to_all(
        spread(by_z).reshape(members, 16, 2, HERE, SPECTRA),
        ("x_lo", "y", "x_hi"),
        split_axis=0,
        concat_axis=0,
        tiled=True,
    ).reshape(CHIPS, *BLOCK)
    swapped = lax.ppermute(stack_for_swap(blocks), "core", [(0, 1), (1, 0)])

    def same(back):
        return lambda chip, core: ((chip + CHIPS - back) % CHIPS, 2 * back)

    def crossed(back):
        return lambda chip, core: (back - 1, 2 * back - 1 + 2 * core)

    out = correlate(plan, blocks, blocks, [same(back) for back in range(5)])
    out = correlate(
        plan,
        blocks,
        swapped,
        [crossed(back) for back in range(1, 4)] + [lambda chip, core: (3, 7 - 6 * core)],
        out,
    )
    return out[None, :, None]


def solution(mesh):
    fine = Mesh(mesh.devices.reshape(2, 4, 2, 2, 16), ("x_lo", "y", "core", "x_hi", "z"))
    grp, dev = ("x_lo", "y", "core"), ("x_hi", "z")
    return jax.shard_map(
        per_device,
        mesh=fine,
        in_specs=(P(None, grp + dev, None), P(), P(grp, None)),
        out_specs=P(grp, None, dev, None, None, None),
        check_vma=False,
    )
```

```python
import math

import jax
import jax.numpy as jnp
import numpy as np
from jax import lax
from jax.experimental import pallas as pl
from jax.experimental.pallas import tpu as pltpu
from jax.sharding import Mesh, PartitionSpec as P

F = 32
TAPS = 4
SPECTRA = 128
FRAMES = 131
HERE = 8
LANES = 128
TILES = 33
ROUNDS = 9
BLK = 256
CHIPS = 8
BLOCK = (32, 2, HERE, SPECTRA)


def dft_table():
    f = np.arange(F)[:, None]
    n = np.arange(F)[None, :]
    angle = 2.0 * math.pi * ((f * n) % F) / F
    cosine = np.tile(np.cos(angle), (1, TAPS))
    sine = np.tile(np.sin(angle), (1, TAPS))
    real_rows = np.concatenate([cosine, sine], axis=1)
    imag_rows = np.concatenate([-sine, cosine], axis=1)
    return np.concatenate([real_rows, imag_rows], axis=0).astype(np.float32)


def split(x):
    high = x.astype(jnp.bfloat16)
    low = (x - high.astype(jnp.float32)).astype(jnp.bfloat16)
    return high, low


def nt(a, b):
    return lax.dot_general(a, b, (((1,), (1,)), ((), ())), preferred_element_type=jnp.float32)


def spectra_kernel(v_ref, taps_ref, table_ref, out_ref, rows, placed):
    for c in range(2):
        for q in range(TILES - 1):
            rows[c, q * HERE : (q + 1) * HERE, :] = v_ref[c, :, q * LANES : (q + 1) * LANES]
        rows[c, (TILES - 1) * HERE :, : FRAMES * F - (TILES - 1) * LANES] = v_ref[
            c, :, (TILES - 1) * LANES :
        ]
    taps = taps_ref[...]
    tap_row = jnp.concatenate([taps[p : p + 1, :] for p in range(TAPS)], axis=1)
    weights = table_ref[...] * jnp.concatenate([tap_row, tap_row], axis=1)
    w_high, w_low = split(weights)
    w_both = jnp.concatenate([w_high, w_low], axis=0)
    lane = lax.broadcasted_iota(jnp.int32, (F, LANES), 1)
    for i in range(HERE):
        halves = []
        for c in range(2):
            here = rows[c, pl.ds(i, 32, stride=HERE), :]
            after = rows[c, pl.ds(i + HERE, 32, stride=HERE), :]
            parts = [here]
            for j in range(1, 4):
                parts.append(pltpu.roll(jnp.where(lane < F * j, after, here), LANES - F * j, 1))
            halves.append(jnp.concatenate(parts, axis=0))
        x_high, x_low = split(jnp.concatenate(halves, axis=1))
        both = nt(w_both, x_high)
        result = both[: 2 * F] + both[2 * F :] + nt(w_high, x_low)
        placed[pl.ds(i, F, stride=2 * HERE), :] = result[:F]
        placed[pl.ds(HERE + i, F, stride=2 * HERE), :] = result[F:]
    values = placed[...].astype(jnp.bfloat16).reshape(2, 16, 2, HERE, SPECTRA)
    out_ref[:, 0] = values[0]
    out_ref[:, 1] = values[1]


def compute_spectra(voltage, filter_taps):
    return pl.pallas_call(
        spectra_kernel,
        out_shape=pltpu.VMEM((16, 2, 2, HERE, SPECTRA), jnp.bfloat16),
        in_specs=[pl.BlockSpec(memory_space=pltpu.VMEM)] * 3,
        out_specs=pl.BlockSpec(memory_space=pltpu.VMEM),
        scratch_shapes=[
            pltpu.VMEM((2, TILES * HERE, LANES), jnp.float32),
            pltpu.VMEM((F * 2 * HERE, SPECTRA), jnp.float32),
        ],
        cost_estimate=pl.CostEstimate(flops=10**8, bytes_accessed=400000, transcendentals=0),
        name="spectra",
    )(voltage, filter_taps, jnp.asarray(dft_table()))


def in_vmem(x):
    return pltpu.with_memory_space_constraint(x, pltpu.VMEM)


def spread_kernel(by_z_ref, out_ref):
    for x_hi in range(2):
        part = by_z_ref[:, x_hi]
        for chip in range(CHIPS):
            out_ref[chip, x_hi] = part


def spread(by_z):
    return pl.pallas_call(
        spread_kernel,
        out_shape=pltpu.VMEM((CHIPS, 2, 16, 2, HERE, SPECTRA), jnp.bfloat16),
        in_specs=[pl.BlockSpec(memory_space=pltpu.VMEM)],
        out_specs=pl.BlockSpec(memory_space=pltpu.VMEM),
        name="spread",
    )(in_vmem(by_z))


def my_chip():
    return 4 * lax.axis_index("x_lo") + lax.axis_index("y")


def stack_kernel(blocks_ref, out_ref):
    chip, core = my_chip(), lax.axis_index("core")
    for back in range(1, 4):
        out_ref[back - 1] = blocks_ref[(chip + CHIPS - back) % CHIPS]
    out_ref[3] = blocks_ref[(chip + 4 * core) % CHIPS]


def stack_for_swap(blocks):
    return pl.pallas_call(
        stack_kernel,
        out_shape=pltpu.VMEM((4, *BLOCK), jnp.bfloat16),
        in_specs=[pl.BlockSpec(memory_space=pltpu.VMEM)],
        out_specs=pl.BlockSpec(memory_space=pltpu.VMEM),
        name="stack_for_swap",
    )(in_vmem(blocks))


def correlate(plan, blocks, partners, entries, before=None):
    count = len(entries)

    def kernel(plan_ref, blocks_ref, ref, *rest):
        out_ref, staged, sems = rest[-3:]
        chosen = plan_ref[...]
        places = lax.broadcasted_iota(jnp.int32, chosen.shape, 1)
        place = (my_chip(), lax.axis_index("core"))
        own = blocks_ref[place[0]]
        left = jnp.concatenate(
            [own[:, 0].reshape(BLK, SPECTRA), own[:, 1].reshape(BLK, SPECTRA)], axis=1
        )
        copies = []
        for b, entry in enumerate(entries):
            index, wanted = entry(*place)
            real_part = ref[index, :, 0].reshape(BLK, SPECTRA)
            imag_part = ref[index, :, 1].reshape(BLK, SPECTRA)
            scale = 1.0 / SPECTRA
            staged[b, 0] = (
                nt(left, jnp.concatenate([real_part, imag_part], axis=1)) * scale
            ).astype(jnp.bfloat16)
            staged[b, 1] = (
                nt(left, jnp.concatenate([-imag_part, real_part], axis=1)) * scale
            ).astype(jnp.bfloat16)
            slot = jnp.sum(jnp.where(chosen == wanted, places, 0))
            copy = pltpu.make_async_copy(staged.at[b], out_ref.at[slot], sems.at[b])
            copy.start()
            copies.append(copy)
        for copy in copies:
            copy.wait()

    operands = [in_vmem(plan), in_vmem(blocks), in_vmem(partners)]
    in_specs = [pl.BlockSpec(memory_space=pltpu.VMEM)] * len(operands)
    aliases = {}
    if before is not None:
        aliases = {len(operands): 0}
        operands.append(before)
        in_specs.append(pl.BlockSpec(memory_space=pl.ANY))
    return pl.pallas_call(
        kernel,
        out_shape=jax.ShapeDtypeStruct((ROUNDS, 2, BLK, BLK), jnp.bfloat16),
        in_specs=in_specs,
        out_specs=pl.BlockSpec(memory_space=pl.ANY),
        scratch_shapes=[
            pltpu.VMEM((count, 2, BLK, BLK), jnp.bfloat16),
            pltpu.SemaphoreType.DMA((count,)),
        ],
        input_output_aliases=aliases,
        cost_estimate=pl.CostEstimate(
            flops=count * 2**26, bytes_accessed=count * 400000, transcendentals=0
        ),
        name="correlate",
    )(*operands)


def per_device(voltage, filter_taps, plan):
    spectra = compute_spectra(voltage, filter_taps)
    by_z = lax.all_to_all(spectra, "z", split_axis=0, concat_axis=0, tiled=True)
    members = CHIPS * 2
    blocks = lax.all_to_all(
        spread(by_z).reshape(members, 16, 2, HERE, SPECTRA),
        ("x_lo", "y", "x_hi"),
        split_axis=0,
        concat_axis=0,
        tiled=True,
    ).reshape(CHIPS, *BLOCK)
    swapped = lax.ppermute(stack_for_swap(blocks), "core", [(0, 1), (1, 0)])

    def same(back):
        return lambda chip, core: ((chip + CHIPS - back) % CHIPS, 2 * back)

    def crossed(back):
        return lambda chip, core: (back - 1, 2 * back - 1 + 2 * core)

    out = correlate(plan, blocks, blocks, [same(back) for back in range(5)])
    out = correlate(
        plan,
        blocks,
        swapped,
        [crossed(back) for back in range(1, 4)] + [lambda chip, core: (3, 7 - 6 * core)],
        out,
    )
    return out[None, :, None]


def solution(mesh):
    fine = Mesh(mesh.devices.reshape(2, 4, 2, 2, 16), ("x_lo", "y", "core", "x_hi", "z"))
    grp, dev = ("x_lo", "y", "core"), ("x_hi", "z")
    return jax.shard_map(
        per_device,
        mesh=fine,
        in_specs=(P(None, grp + dev, None), P(), P(grp, None)),
        out_specs=P(grp, None, dev, None, None, None),
        check_vma=False,
    )
```

```python
import math

import jax
import jax.numpy as jnp
import numpy as np
from jax import lax
from jax.experimental import pallas as pl
from jax.experimental.pallas import tpu as pltpu
from jax.sharding import Mesh, PartitionSpec as P

F = 32
TAPS = 4
SPECTRA = 128
FRAMES = 131
HERE = 8
LANES = 128
TILES = 33
ROUNDS = 9
BLK = 256
CHIPS = 8
BLOCK = (32, 2, HERE, SPECTRA)


def dft_table():
    f = np.arange(F)[:, None]
    n = np.arange(F)[None, :]
    angle = 2.0 * math.pi * ((f * n) % F) / F
    cosine = np.tile(np.cos(angle), (1, TAPS))
    sine = np.tile(np.sin(angle), (1, TAPS))
    real_rows = np.concatenate([cosine, sine], axis=1)
    imag_rows = np.concatenate([-sine, cosine], axis=1)
    return np.concatenate([real_rows, imag_rows], axis=0).astype(np.float32)


def split(x):
    high = x.astype(jnp.bfloat16)
    low = (x - high.astype(jnp.float32)).astype(jnp.bfloat16)
    return high, low


def nt(a, b):
    return lax.dot_general(a, b, (((1,), (1,)), ((), ())), preferred_element_type=jnp.float32)


def spectra_kernel(v_ref, taps_ref, table_ref, out_ref, rows, placed):
    for c in range(2):
        for q in range(TILES - 1):
            rows[c, q * HERE : (q + 1) * HERE, :] = v_ref[c, :, q * LANES : (q + 1) * LANES]
        rows[c, (TILES - 1) * HERE :, : FRAMES * F - (TILES - 1) * LANES] = v_ref[
            c, :, (TILES - 1) * LANES :
        ]
    taps = taps_ref[...]
    tap_row = jnp.concatenate([taps[p : p + 1, :] for p in range(TAPS)], axis=1)
    weights = table_ref[...] * jnp.concatenate([tap_row, tap_row], axis=1)
    w_high, w_low = split(weights)
    w_both = jnp.concatenate([w_high, w_low], axis=0)
    lane = lax.broadcasted_iota(jnp.int32, (F, LANES), 1)
    for i in range(HERE):
        halves = []
        for c in range(2):
            here = rows[c, pl.ds(i, 32, stride=HERE), :]
            after = rows[c, pl.ds(i + HERE, 32, stride=HERE), :]
            parts = [here]
            for j in range(1, 4):
                parts.append(pltpu.roll(jnp.where(lane < F * j, after, here), LANES - F * j, 1))
            halves.append(jnp.concatenate(parts, axis=0))
        x_high, x_low = split(jnp.concatenate(halves, axis=1))
        both = nt(w_both, x_high)
        result = both[: 2 * F] + both[2 * F :] + nt(w_high, x_low)
        placed[pl.ds(i, F, stride=2 * HERE), :] = result[:F]
        placed[pl.ds(HERE + i, F, stride=2 * HERE), :] = result[F:]
    values = placed[...].astype(jnp.bfloat16).reshape(2, 16, 2, HERE, SPECTRA)
    out_ref[:, 0] = values[0]
    out_ref[:, 1] = values[1]


def compute_spectra(voltage, filter_taps):
    return pl.pallas_call(
        spectra_kernel,
        out_shape=pltpu.VMEM((16, 2, 2, HERE, SPECTRA), jnp.bfloat16),
        in_specs=[pl.BlockSpec(memory_space=pltpu.VMEM)] * 3,
        out_specs=pl.BlockSpec(memory_space=pltpu.VMEM),
        scratch_shapes=[
            pltpu.VMEM((2, TILES * HERE, LANES), jnp.float32),
            pltpu.VMEM((F * 2 * HERE, SPECTRA), jnp.float32),
        ],
        cost_estimate=pl.CostEstimate(flops=10**8, bytes_accessed=400000, transcendentals=0),
        name="spectra",
    )(voltage, filter_taps, jnp.asarray(dft_table()))


def in_vmem(x):
    return pltpu.with_memory_space_constraint(x, pltpu.VMEM)


def spread_kernel(by_z_ref, out_ref):
    for x_hi in range(2):
        part = by_z_ref[:, x_hi]
        for chip in range(CHIPS):
            out_ref[chip, x_hi] = part


def spread(by_z):
    return pl.pallas_call(
        spread_kernel,
        out_shape=pltpu.VMEM((CHIPS, 2, 16, 2, HERE, SPECTRA), jnp.bfloat16),
        in_specs=[pl.BlockSpec(memory_space=pltpu.VMEM)],
        out_specs=pl.BlockSpec(memory_space=pltpu.VMEM),
        name="spread",
    )(in_vmem(by_z))


def my_chip():
    return 4 * lax.axis_index("x_lo") + lax.axis_index("y")


def stack_kernel(blocks_ref, out_ref):
    chip, core = my_chip(), lax.axis_index("core")
    for back in range(1, 4):
        out_ref[back - 1] = blocks_ref[(chip + CHIPS - back) % CHIPS]
    out_ref[3] = blocks_ref[(chip + 4 * core) % CHIPS]


def stack_for_swap(blocks):
    return pl.pallas_call(
        stack_kernel,
        out_shape=pltpu.VMEM((4, *BLOCK), jnp.bfloat16),
        in_specs=[pl.BlockSpec(memory_space=pltpu.VMEM)],
        out_specs=pl.BlockSpec(memory_space=pltpu.VMEM),
        name="stack_for_swap",
    )(in_vmem(blocks))


def correlate(plan, own, partners, entries, before=None):
    count = len(entries)

    def kernel(plan_ref, left_ref, ref, *rest):
        staged, sems = rest[-2:]
        out_ref = rest[-3] if before is not None else rest[0]
        chosen = plan_ref[...]
        places = lax.broadcasted_iota(jnp.int32, chosen.shape, 1)
        place = (my_chip(), lax.axis_index("core"))
        if before is None:
            own = left_ref[place[0]]
            left = jnp.concatenate(
                [own[:, 0].reshape(BLK, SPECTRA), own[:, 1].reshape(BLK, SPECTRA)], axis=1
            )
            rest[1][...] = left
        else:
            left = left_ref[...]
        copies = []
        for b, entry in enumerate(entries):
            index, wanted = entry(*place)
            real_part = ref[index, :, 0].reshape(BLK, SPECTRA)
            imag_part = ref[index, :, 1].reshape(BLK, SPECTRA)
            scale = 1.0 / SPECTRA
            staged[b, 0] = (
                nt(left, jnp.concatenate([real_part, imag_part], axis=1)) * scale
            ).astype(jnp.bfloat16)
            staged[b, 1] = (
                nt(left, jnp.concatenate([-imag_part, real_part], axis=1)) * scale
            ).astype(jnp.bfloat16)
            slot = jnp.sum(jnp.where(chosen == wanted, places, 0))
            copy = pltpu.make_async_copy(staged.at[b], out_ref.at[slot], sems.at[b])
            copy.start()
            copies.append(copy)
        for copy in copies:
            copy.wait()

    operands = [in_vmem(plan), in_vmem(own), in_vmem(partners)]
    in_specs = [pl.BlockSpec(memory_space=pltpu.VMEM)] * len(operands)
    aliases = {}
    out_shape = jax.ShapeDtypeStruct((ROUNDS, 2, BLK, BLK), jnp.bfloat16)
    out_specs = pl.BlockSpec(memory_space=pl.ANY)
    if before is None:
        out_shape = (out_shape, pltpu.VMEM((BLK, 2 * SPECTRA), jnp.bfloat16))
        out_specs = (out_specs, pl.BlockSpec(memory_space=pltpu.VMEM))
    if before is not None:
        aliases = {len(operands): 0}
        operands.append(before)
        in_specs.append(pl.BlockSpec(memory_space=pl.ANY))
    return pl.pallas_call(
        kernel,
        out_shape=out_shape,
        in_specs=in_specs,
        out_specs=out_specs,
        scratch_shapes=[
            pltpu.VMEM((count, 2, BLK, BLK), jnp.bfloat16),
            pltpu.SemaphoreType.DMA((count,)),
        ],
        input_output_aliases=aliases,
        cost_estimate=pl.CostEstimate(
            flops=count * 2**26, bytes_accessed=count * 400000, transcendentals=0
        ),
        name="correlate",
    )(*operands)


def per_device(voltage, filter_taps, plan):
    spectra = compute_spectra(voltage, filter_taps)
    by_z = lax.all_to_all(spectra, "z", split_axis=0, concat_axis=0, tiled=True)
    members = CHIPS * 2
    blocks = lax.all_to_all(
        spread(by_z).reshape(members, 16, 2, HERE, SPECTRA),
        ("x_lo", "y", "x_hi"),
        split_axis=0,
        concat_axis=0,
        tiled=True,
    ).reshape(CHIPS, *BLOCK)
    swapped = lax.ppermute(stack_for_swap(blocks), "core", [(0, 1), (1, 0)])

    def same(back):
        return lambda chip, core: ((chip + CHIPS - back) % CHIPS, 2 * back)

    def crossed(back):
        return lambda chip, core: (back - 1, 2 * back - 1 + 2 * core)

    out, left = correlate(plan, blocks, blocks, [same(back) for back in range(5)])
    out = correlate(
        plan,
        left,
        swapped,
        [crossed(back) for back in range(1, 4)] + [lambda chip, core: (3, 7 - 6 * core)],
        out,
    )
    return out[None, :, None]


def solution(mesh):
    fine = Mesh(mesh.devices.reshape(2, 4, 2, 2, 16), ("x_lo", "y", "core", "x_hi", "z"))
    grp, dev = ("x_lo", "y", "core"), ("x_hi", "z")
    return jax.shard_map(
        per_device,
        mesh=fine,
        in_specs=(P(None, grp + dev, None), P(), P(grp, None)),
        out_specs=P(grp, None, dev, None, None, None),
        check_vma=False,
    )
```
